128 devices in a mesh: snp: 16 (over z_lo, y, core), samp: 8 (over x, z_hi).
Axes of the slice: x: 4, y: 4, z: 4 (z_hi: 2, z_lo: 2; z = z_hi * 2 + z_lo), core: 2. Of those that a mesh axis runs over, the one named last changes fastest.
Arguments:
- genotypes: float32 [16384, 4096], P('snp', 'samp'), may hold values from -1 to 2, as said below
- pcs: float32 [20, 4096], P(None, 'samp'), may hold values from -6 to 6
Outputs:
- kinship: float32 [4096, 4096], P('snp', 'samp')
The draws below stay inside these ranges and needn't reach their ends.
Inputs may be any that keep to these rules, and one draw needn't show every extreme that they name: `genotypes`: observed entries are real-valued dosages from 0 to 2 and -1 marks a missing entry; SNPs whose index is a multiple of 16 are never missing.
All inputs are finite; a program needn't handle non-finite values.
Results may differ from the reference program's by a relative error of at most 0.0015.
Values may be sent and summed in bfloat16 or wider, within the bound.
A program may use at most 64 MiB of HBM per device.

```python
import jax
import jax.numpy as jnp
from jax import lax

K = 20
SNPS = 16384
N = 4096


population_groups = 6


family_members = 4


def families(key):
    order = jax.random.permutation(jax.random.fold_in(key, 5), N)
    return order // family_members


def population(key):
    family = families(key)
    family_groups = jax.random.randint(jax.random.fold_in(key, 7), (N // family_members,), 0, population_groups)
    return family_groups[family]


def allele_copy(key, salt, chosen, shared_allele):
    fresh = (jax.random.randint(jax.random.fold_in(key, salt), (SNPS, N), 0, 1000) < chosen).astype(jnp.int32)
    inherit = jax.random.randint(jax.random.fold_in(key, salt + 1), (SNPS, N), 0, 2) == 1
    return jnp.where(inherit, shared_allele, fresh)


def draw_genotypes(key, part):
    groups = population(key)
    family = families(key)
    limits = jax.random.randint(jax.random.fold_in(key, 11), (SNPS, population_groups), 1, 500)
    chosen = jnp.take(limits, groups, axis=1)
    family_chosen = jnp.take(limits, jax.random.randint(jax.random.fold_in(key, 7), (N // family_members,), 0, population_groups), axis=1)
    shared_first = (jax.random.randint(jax.random.fold_in(key, 31), (SNPS, N // family_members), 0, 1000) < family_chosen).astype(jnp.int32)
    shared_second = (jax.random.randint(jax.random.fold_in(key, 37), (SNPS, N // family_members), 0, 1000) < family_chosen).astype(jnp.int32)
    first = allele_copy(key, 13, chosen, jnp.take(shared_first, family, axis=1))
    second = allele_copy(key, 17, chosen, jnp.take(shared_second, family, axis=1))
    hard = (first + second).astype(jnp.float32)
    noise = jax.random.uniform(jax.random.fold_in(key, 41), (SNPS, N), jnp.float32, -0.45, 0.45)
    soft = jnp.clip(hard + noise, 0.0, 2.0)
    sample_rate = jax.random.randint(jax.random.fold_in(key, 43), (1, N), 0, 257)
    lost = jax.random.randint(jax.random.fold_in(key, 19), (SNPS, N), 0, 1024) < sample_rate
    snp_index = jnp.arange(SNPS)[:, None]
    lost = jnp.logical_and(lost, snp_index % 16 != 0)
    return jnp.where(lost, -1.0, soft).astype(jnp.float32)


def draw_pcs(key, part):
    groups = population(key)
    loadings = jax.random.normal(jax.random.fold_in(key, 21), (K, population_groups), jnp.float32)
    centers = jnp.take(loadings, groups, axis=1)
    noise = jax.random.normal(jax.random.fold_in(key, 23), (K, N), jnp.float32)
    values = centers + 0.5 * noise
    return jnp.clip(values, -6.0, 6.0).astype(jnp.float32)


def setup_inputs(seed: int = 0) -> dict:
    streams_of = jax.random.split(jax.random.key(seed), 3)
    return {
        "genotypes": draw_genotypes(jax.random.fold_in(streams_of[2], 71), 0),
        "pcs": draw_pcs(jax.random.fold_in(streams_of[2], 71), 0),
    }


def reference(genotypes, pcs):
    count = pcs.shape[1]
    design = jnp.concatenate([jnp.ones((1, count), jnp.float32), pcs.astype(jnp.float32)], axis=0)
    observed = genotypes >= 0.0
    dosage = jnp.where(observed, genotypes, 0.0).astype(jnp.float32)
    design_gram = jnp.dot(design, design.T, precision=lax.Precision.HIGHEST)
    cross = jnp.dot(design, dosage.T, precision=lax.Precision.HIGHEST)
    factor = jnp.linalg.cholesky(design_gram)
    coef = jax.scipy.linalg.cho_solve((factor, True), cross)
    fitted = jnp.dot(coef.T, design, precision=lax.Precision.HIGHEST)
    freq = jnp.clip(0.5 * fitted, 0.02, 0.98)
    resid = jnp.where(observed, dosage - 2.0 * freq, 0.0).astype(jnp.bfloat16)
    spread = jnp.where(observed, jnp.sqrt(freq * (1.0 - freq)), 0.0).astype(jnp.bfloat16)
    numer = jnp.dot(resid.T.astype(jnp.float32), resid.astype(jnp.float32), preferred_element_type=jnp.float32)
    denom = jnp.dot(spread.T.astype(jnp.float32), spread.astype(jnp.float32), preferred_element_type=jnp.float32)
    return numer / (4.0 * denom)
```

```python
import jax
import jax.numpy as jnp
from jax import lax
from jax.sharding import PartitionSpec as P

AXES = ("snp", "samp")
HIGH = lax.Precision.HIGHEST
MISSING = 4.0
PAD = 32


def decode(snp, samp):
    return samp // 2, (snp // 2) % 4, samp % 2, snp // 8, snp % 2


def encode(x, y, zh, zl, c):
    return ((zl * 4 + y) * 2 + c) * 8 + x * 2 + zh


def pairs(where):
    return [(s * 8 + j, encode(*where(*decode(s, j)))) for s in range(16) for j in range(8)]


def move(value, where):
    return lax.ppermute(value, AXES, pairs(where))


def from_x(value, d):
    return move(value, lambda x, y, zh, zl, c: ((x - d) % 4, y, zh, zl, c))


def from_z(value, d):
    def where(x, y, zh, zl, c):
        z = (zh * 2 + zl - d) % 4
        return x, y, z // 2, z % 2, c

    return move(value, where)


def flip(value):
    return move(value, lambda x, y, zh, zl, c: (x, y, zh, zl, 1 - c))


def from_y(value, d):
    return move(value, lambda x, y, zh, zl, c: (x, (y - d) % 4, zh, zl, c))


def rows_at(y, zh):
    return zh * ((y % 2) * 2 + y // 2) + (1 - zh) * (y ^ (y // 2))


def to_owner(value):
    def where(x, y, zh, zl, c):
        xi = rows_at(y, zh)
        return x, (xi % 2) * 2 + zh, c, xi // 2, zl

    return move(value, where)


def split3(a):
    hi = lax.reduce_precision(a, 8, 7)
    mid = lax.reduce_precision(a - hi, 8, 7)
    low = (a - hi) - mid
    return [v.astype(jnp.bfloat16) for v in (hi, mid, low)]


def left_terms(a):
    a1, a2, a3 = split3(a)
    return jnp.concatenate([a1, a1, a2, a1, a3, a2], axis=0)


def right_terms(b):
    b1, b2, b3 = split3(b)
    return jnp.concatenate([b1, b2, b1, b3, b1, b2], axis=0)


def frequencies(coef6, design6):
    fitted = lax.dot_general(coef6, design6, (((0,), (0,)), ((), ())), preferred_element_type=jnp.float32)
    return jnp.clip(0.5 * fitted, 0.02, 0.98)


def open_code(code, freq):
    seen = code < 3.0
    resid = jnp.where(seen, code, jnp.zeros_like(code))
    spread = jnp.where(seen, jnp.sqrt(freq * (1.0 - freq)), 0.0).astype(jnp.bfloat16)
    return resid, spread


def gram(a, b):
    return lax.dot_general(a, b, (((0,), (0,)), ((), ())), preferred_element_type=jnp.float32)


def body(genotypes, pcs):
    x, y, zh, zl, c = decode(lax.axis_index("snp"), lax.axis_index("samp"))
    here = genotypes.shape[1]
    half = here // 2
    count = pcs.shape[0] + 1
    design = jnp.concatenate([jnp.ones((1, here), jnp.float32), pcs, jnp.zeros((PAD - count, here), jnp.float32)], axis=0)
    design_zh = jnp.stack([design, from_z(design, 2)])
    designs = [design_zh] + [from_x(design_zh, d) for d in (1, 2, 3)]
    observed = genotypes >= 0.0
    dosage = jnp.where(observed, genotypes, 0.0)
    cross = lax.dot_general(design, dosage, (((1,), (1,)), ((), ())), precision=HIGH)
    cross = cross + from_z(cross, 2)
    cross = (cross + from_x(cross, 2)) + (from_x(cross, 1) + from_x(cross, 3))
    total = None
    for d in designs:
        for k in range(2):
            part = lax.dot_general(d[k], d[k], (((1,), (1,)), ((), ())), precision=HIGH)
            total = part if total is None else total + part
    factor = jnp.linalg.cholesky(total[:count, :count])
    inverse = jax.scipy.linalg.cho_solve((factor, True), jnp.eye(count, dtype=jnp.float32))
    inverse = jnp.pad(inverse, ((0, PAD - count), (0, PAD - count)))
    coef = jnp.dot(inverse, cross, precision=HIGH)
    coef_far = from_z(coef, 1)
    near6 = left_terms(coef)
    far6 = left_terms(coef_far)
    freq = frequencies(near6, right_terms(design))
    code = jnp.where(observed, dosage - 2.0 * freq, MISSING).astype(jnp.bfloat16)
    rows_near = lax.dynamic_slice(code, (0, zl * half), (code.shape[0], half))
    up, down = from_z(code, 1), from_z(code, 3)
    rows = [[rows_near] + [from_x(rows_near, d) for d in (1, 2, 3)]]
    far_same = jnp.where(zl == 0, up, down)
    far_other = jnp.where(zl == 0, down, up)
    rows_far = lax.dynamic_slice(far_same, (0, zl * half), (code.shape[0], half))
    rows.append([rows_far] + [from_x(rows_far, d) for d in (1, 2, 3)])
    across = from_z(lax.optimization_barrier((code, up, down))[0], 2)

    def in_order(a, b, axis):
        return jnp.concatenate([jnp.where(zh == 0, a, b), jnp.where(zh == 0, b, a)], axis=axis)

    col_design6 = right_terms(in_order(design_zh[0], design_zh[1], 1))
    near_resid, near_spread = open_code(in_order(code, across, 1), frequencies(near6, col_design6))
    far_resid, far_spread = open_code(in_order(far_same, far_other, 1), frequencies(far6, col_design6))
    col_resid = jnp.concatenate([near_resid, far_resid], axis=0)
    col_spread = jnp.concatenate([near_spread, far_spread], axis=0)
    row_resid, row_spread = [], []
    for d in range(4):
        part = right_terms(lax.dynamic_slice(designs[d][0], (0, zl * half), (PAD, half)))
        n_resid, n_spread = open_code(rows[0][d], frequencies(near6, part))
        f_resid, f_spread = open_code(rows[1][d], frequencies(far6, part))
        row_resid.append(jnp.concatenate([n_resid, f_resid], axis=0))
        row_spread.append(jnp.concatenate([n_spread, f_spread], axis=0))
    row_resid = jnp.stack(row_resid)
    row_spread = jnp.stack(row_spread)
    sums = None
    for step in (2, 1, 3, 0):
        d = (rows_at((y + step) % 4, zh) - x) % 4
        numer = gram(lax.dynamic_index_in_dim(row_resid, d, 0, False), col_resid)
        denom = gram(lax.dynamic_index_in_dim(row_spread, d, 0, False), col_spread)
        both = jnp.stack([numer, denom])
        keep = lax.dynamic_slice(both, (0, 0, c * here), (2, half, here))
        give = lax.dynamic_slice(both, (0, 0, (1 - c) * here), (2, half, here))
        merged = keep + flip(give)
        if step:
            low = merged[1].astype(jnp.bfloat16)
            top = merged[0] * (low.astype(jnp.float32) / merged[1])
            merged = from_y(jnp.stack([top.astype(jnp.bfloat16), low]), 4 - step).astype(jnp.float32)
        sums = merged if sums is None else sums + merged
    return to_owner(sums[0] / (4.0 * sums[1]))


def solution(mesh):
    in_specs = (P("snp", "samp"), P(None, "samp"))
    out_specs = P("snp", "samp")
    return jax.shard_map(body, mesh=mesh, in_specs=in_specs, out_specs=out_specs, check_vma=False)
```

```python
import functools

import jax
import jax.numpy as jnp
from jax import lax
from jax.experimental import pallas as pl
from jax.experimental.pallas import tpu as pltpu
from jax.sharding import PartitionSpec as P

AXES = ("snp", "samp")
HIGH = lax.Precision.HIGHEST
MISSING = 4.0
PAD = 32
TILE = 256


def decode(snp, samp):
    return samp // 2, (snp // 2) % 4, samp % 2, snp // 8, snp % 2


def encode(x, y, zh, zl, c):
    return ((zl * 4 + y) * 2 + c) * 8 + x * 2 + zh


def pairs(where):
    return [(s * 8 + j, encode(*where(*decode(s, j)))) for s in range(16) for j in range(8)]


def move(value, where):
    return lax.ppermute(value, AXES, pairs(where))


def from_x(value, d):
    return move(value, lambda x, y, zh, zl, c: ((x - d) % 4, y, zh, zl, c))


def from_z(value, d):
    def where(x, y, zh, zl, c):
        z = (zh * 2 + zl - d) % 4
        return x, y, z // 2, z % 2, c

    return move(value, where)


def flip(value):
    return move(value, lambda x, y, zh, zl, c: (x, y, zh, zl, 1 - c))


def from_y(value, d):
    return move(value, lambda x, y, zh, zl, c: (x, (y - d) % 4, zh, zl, c))


def rows_at(y, zh):
    return zh * ((y % 2) * 2 + y // 2) + (1 - zh) * (y ^ (y // 2))


def to_owner(value):
    def where(x, y, zh, zl, c):
        xi = rows_at(y, zh)
        return x, (xi % 2) * 2 + zh, c, xi // 2, zl

    return move(value, where)


LEFT = (0, 0, 1, 0, 2, 1)
RIGHT = (0, 1, 0, 2, 0, 1)


def terms_kernel(order, value, out):
    a = value[...]
    parts = []
    for _ in range(3):
        parts.append(a.astype(jnp.bfloat16))
        a = a - parts[-1].astype(jnp.float32)
    for k, part in enumerate(order):
        out[k * PAD : (k + 1) * PAD, :] = parts[part]


def terms(value, order):
    rows, columns = value.shape
    return pl.pallas_call(
        functools.partial(terms_kernel, order),
        out_shape=jax.ShapeDtypeStruct((rows * len(order), columns), jnp.bfloat16),
        compiler_params=pltpu.CompilerParams(vmem_limit_bytes=4 << 20),
        name="terms",
    )(value)


def frequencies(coef6, design6):
    fitted = lax.dot_general(coef6, design6, (((0,), (0,)), ((), ())), preferred_element_type=jnp.float32)
    return jnp.clip(0.5 * fitted, 0.02, 0.98)


def spread_kernel(left, right, out):
    @pl.loop(0, right.shape[1] // TILE)
    def _(k):
        at = pl.ds(pl.multiple_of(k * TILE, TILE), TILE)
        freq = frequencies(left[...], right[:, at])
        out[:, at] = jnp.sqrt(freq * (1.0 - freq)).astype(jnp.bfloat16)


def spreads(left, right):
    rows, columns = left.shape[1], right.shape[1]
    return pl.pallas_call(
        spread_kernel,
        grid=(rows // TILE,),
        in_specs=[
            pl.BlockSpec((left.shape[0], TILE), lambda i: (0, i)),
            pl.BlockSpec(right.shape, lambda i: (0, 0)),
        ],
        out_specs=pl.BlockSpec((TILE, columns), lambda i: (i, 0)),
        out_shape=jax.ShapeDtypeStruct((rows, columns), jnp.bfloat16),
        compiler_params=pltpu.CompilerParams(vmem_limit_bytes=12 << 20),
        name="spreads",
    )(left, right)


def open_kernel(code, raw, resid, spread):
    seen = code[...] < 3.0
    resid[...] = jnp.where(seen, code[...], jnp.zeros_like(code))
    spread[...] = jnp.where(seen, raw[...], jnp.zeros_like(code))


def open_code(code, raw, which):
    rows, columns = code.shape
    block = pl.BlockSpec((TILE, columns), lambda i: (i, 0))
    return pl.pallas_call(
        open_kernel,
        grid=(rows // TILE,),
        in_specs=[block, pl.BlockSpec((TILE, columns), lambda i: (i, which))],
        out_specs=[block, block],
        out_shape=[jax.ShapeDtypeStruct(code.shape, jnp.bfloat16)] * 2,
        compiler_params=pltpu.CompilerParams(vmem_limit_bytes=8 << 20),
        name="open_code",
    )(code, raw)


def gram(a, b):
    return lax.dot_general(a, b, (((0,), (0,)), ((), ())), preferred_element_type=jnp.float32)


def body(genotypes, pcs):
    x, y, zh, zl, c = decode(lax.axis_index("snp"), lax.axis_index("samp"))
    here = genotypes.shape[1]
    half = here // 2
    count = pcs.shape[0] + 1
    design = jnp.concatenate([jnp.ones((1, here), jnp.float32), pcs, jnp.zeros((PAD - count, here), jnp.float32)], axis=0)
    design_zh = jnp.stack([design, from_z(design, 2)])
    designs = [design_zh] + [from_x(design_zh, d) for d in (1, 2, 3)]
    observed = genotypes >= 0.0
    dosage = jnp.where(observed, genotypes, 0.0)
    cross = lax.dot_general(design, dosage, (((1,), (1,)), ((), ())), precision=HIGH)
    cross = cross + from_z(cross, 2)
    cross = (cross + from_x(cross, 2)) + (from_x(cross, 1) + from_x(cross, 3))
    total = None
    for d in designs:
        for k in range(2):
            part = lax.dot_general(d[k], d[k], (((1,), (1,)), ((), ())), precision=HIGH)
            total = part if total is None else total + part
    factor = jnp.linalg.cholesky(total[:count, :count])
    inverse = jax.scipy.linalg.cho_solve((factor, True), jnp.eye(count, dtype=jnp.float32))
    inverse = jnp.pad(inverse, ((0, PAD - count), (0, PAD - count)))
    coef = jnp.dot(inverse, cross, precision=HIGH)
    coef_far = from_z(coef, 1)

    def in_order(a, b):
        return jnp.concatenate([jnp.where(zh == 0, a, b), jnp.where(zh == 0, b, a)], axis=1)

    def my_half(value):
        return lax.dynamic_slice(value, (0, zl * half), (value.shape[0], half))

    own6 = terms(design, RIGHT)
    all6 = terms(jnp.concatenate([in_order(*designs[0])] + [my_half(d[0]) for d in designs], axis=1), RIGHT)
    near6 = terms(coef, LEFT)
    freq = frequencies(near6, own6)
    code = jnp.where(observed, dosage - 2.0 * freq, MISSING).astype(jnp.bfloat16)
    code, coef_far = lax.optimization_barrier((code, coef_far))
    up, down = from_z(code, 1), from_z(code, 3)
    near_half = my_half(code)
    near_rows = [near_half] + [from_x(near_half, d) for d in (1, 2, 3)]
    raw = spreads(jnp.concatenate([near6, terms(coef_far, LEFT)], axis=1), all6)
    far_same = jnp.where(zl == 0, up, down)
    far_other = jnp.where(zl == 0, down, up)
    far_half = my_half(far_same)
    far_rows = [far_half] + [from_x(far_half, d) for d in (1, 2, 3)]
    across = from_z(lax.optimization_barrier((code, up, down))[0], 2)
    rows = jnp.concatenate([jnp.concatenate(near_rows, axis=1), jnp.concatenate(far_rows, axis=1)], axis=0)
    row_resid, row_spread = open_code(rows, raw, 1)
    columns = jnp.concatenate([in_order(code, across), in_order(far_same, far_other)], axis=0)
    col_resid, col_spread = open_code(columns, raw, 0)

    sums = None
    for step in (2, 1, 3, 0):
        at = (0, (rows_at((y + step) % 4, zh) - x) % 4 * half)
        numer = gram(lax.dynamic_slice(row_resid, at, (rows.shape[0], half)), col_resid)
        denom = gram(lax.dynamic_slice(row_spread, at, (rows.shape[0], half)), col_spread)
        both = jnp.stack([numer, denom])
        keep = lax.dynamic_slice(both, (0, 0, c * here), (2, half, here))
        give = lax.dynamic_slice(both, (0, 0, (1 - c) * here), (2, half, here))
        merged = keep + flip(give)
        if step:
            low = merged[1].astype(jnp.bfloat16)
            top = merged[0] * (low.astype(jnp.float32) / merged[1])
            merged = from_y(jnp.stack([top.astype(jnp.bfloat16), low]), 4 - step).astype(jnp.float32)
        sums = merged if sums is None else sums + merged
    return to_owner(sums[0] / (4.0 * sums[1]))


def solution(mesh):
    in_specs = (P("snp", "samp"), P(None, "samp"))
    out_specs = P("snp", "samp")
    return jax.shard_map(body, mesh=mesh, in_specs=in_specs, out_specs=out_specs, check_vma=False)
```

```python
import functools

import jax
import jax.numpy as jnp
from jax import lax
from jax.experimental import pallas as pl
from jax.experimental.pallas import tpu as pltpu
from jax.sharding import PartitionSpec as P

AXES = ("snp", "samp")
HIGH = lax.Precision.HIGHEST
MISSING = 4.0
PAD = 32
TILE = 256


def decode(snp, samp):
    return samp // 2, (snp // 2) % 4, samp % 2, snp // 8, snp % 2


def encode(x, y, zh, zl, c):
    return ((zl * 4 + y) * 2 + c) * 8 + x * 2 + zh


def pairs(where):
    return [(s * 8 + j, encode(*where(*decode(s, j)))) for s in range(16) for j in range(8)]


def move(value, where):
    return lax.ppermute(value, AXES, pairs(where))


def from_x(value, d):
    return move(value, lambda x, y, zh, zl, c: ((x - d) % 4, y, zh, zl, c))


def from_z(value, d):
    def where(x, y, zh, zl, c):
        z = (zh * 2 + zl - d) % 4
        return x, y, z // 2, z % 2, c

    return move(value, where)


def flip(value):
    return move(value, lambda x, y, zh, zl, c: (x, y, zh, zl, 1 - c))


def from_y(value, d):
    return move(value, lambda x, y, zh, zl, c: (x, (y - d) % 4, zh, zl, c))


def rows_at(y, zh):
    return zh * ((y % 2) * 2 + y // 2) + (1 - zh) * (y ^ (y // 2))


def to_owner(value):
    def where(x, y, zh, zl, c):
        xi = rows_at(y, zh)
        return x, (xi % 2) * 2 + zh, c, xi // 2, zl

    return move(value, where)


LEFT = (0, 0, 1, 0, 2, 1)
RIGHT = (0, 1, 0, 2, 0, 1)


def terms_kernel(order, value, out):
    a = value[...]
    parts = []
    for _ in range(3):
        parts.append(a.astype(jnp.bfloat16))
        a = a - parts[-1].astype(jnp.float32)
    for k, part in enumerate(order):
        out[k * PAD : (k + 1) * PAD, :] = parts[part]


def terms(value, order):
    rows, columns = value.shape
    return pl.pallas_call(
        functools.partial(terms_kernel, order),
        out_shape=jax.ShapeDtypeStruct((rows * len(order), columns), jnp.bfloat16),
        compiler_params=pltpu.CompilerParams(vmem_limit_bytes=4 << 20),
        name="terms",
    )(value)


def frequencies(coef6, design6):
    fitted = lax.dot_general(coef6, design6, (((0,), (0,)), ((), ())), preferred_element_type=jnp.float32)
    return jnp.clip(0.5 * fitted, 0.02, 0.98)


def spread_kernel(left, right, *outs):
    flat = left[...].T
    each = outs[0].shape[1]
    for n, out in enumerate(outs):
        for k in range(0, each, TILE):
            fitted = jnp.dot(flat, right[:, n * each + k : n * each + k + TILE], preferred_element_type=jnp.float32)
            freq = jnp.clip(0.5 * fitted, 0.02, 0.98)
            square = freq * (1.0 - freq)
            out[:, k : k + TILE] = (square * lax.rsqrt(square)).astype(jnp.bfloat16)


def spreads(left, right):
    rows, columns = left.shape[1], right.shape[1] // 2
    return pl.pallas_call(
        spread_kernel,
        grid=(rows // TILE,),
        in_specs=[
            pl.BlockSpec((left.shape[0], TILE), lambda i: (0, i)),
            pl.BlockSpec(right.shape, lambda i: (0, 0)),
        ],
        out_specs=[pl.BlockSpec((TILE, columns), lambda i: (i, 0))] * 2,
        out_shape=[jax.ShapeDtypeStruct((rows, columns), jnp.bfloat16)] * 2,
        compiler_params=pltpu.CompilerParams(vmem_limit_bytes=12 << 20),
        name="spreads",
    )(left, right)


def open_piece(code, raw, resid, spread):
    @pl.loop(0, code.shape[0] // TILE)
    def _(k):
        at = pl.ds(pl.multiple_of(k * TILE, TILE), TILE)
        value = code[at, :]
        seen = value < 3.0
        zero = jnp.zeros_like(value)
        resid[at, :] = jnp.where(seen, value, zero)
        spread[at, :] = jnp.where(seen, raw[at, :], zero)


def open_rows_kernel(*refs):
    raw, resid, spread = refs[8:]
    for k in range(8):
        length, width = refs[k].shape
        at = pl.ds(k // 4 * length, length)
        open_piece(
            refs[k],
            raw.at[at, pl.ds(k % 4 * width, width)],
            resid.at[k % 4, at],
            spread.at[k % 4, at],
        )


def open_columns_kernel(zh, *refs):
    raw, resid, spread = refs[4:]
    for k in range(4):
        length, width = refs[k].shape
        first = zh[0] if k % 2 == 0 else 1 - zh[0]
        at = (pl.ds(k // 2 * length, length), pl.ds(pl.multiple_of(first * width, width), width))
        open_piece(refs[k], raw.at[at], resid.at[at], spread.at[at])


VMEM = pl.BlockSpec(memory_space=pltpu.VMEM)
SMEM = pl.BlockSpec(memory_space=pltpu.SMEM)


def open_code(kernel, shape, scalars, arrays):
    return pl.pallas_call(
        kernel,
        in_specs=[SMEM] * len(scalars) + [VMEM] * len(arrays),
        out_specs=[VMEM] * 2,
        out_shape=[jax.ShapeDtypeStruct(shape, jnp.bfloat16)] * 2,
        compiler_params=pltpu.CompilerParams(vmem_limit_bytes=8 << 20),
        name=kernel.__name__,
    )(*scalars, *arrays)


def gram(a, b):
    return lax.dot_general(a, b, (((0,), (0,)), ((), ())), preferred_element_type=jnp.float32)


def body(genotypes, pcs):
    x, y, zh, zl, c = decode(lax.axis_index("snp"), lax.axis_index("samp"))
    here = genotypes.shape[1]
    half = here // 2
    count = pcs.shape[0] + 1
    design = jnp.concatenate([jnp.ones((1, here), jnp.float32), pcs, jnp.zeros((PAD - count, here), jnp.float32)], axis=0)
    design_zh = jnp.stack([design, from_z(design, 2)])
    designs = [design_zh] + [from_x(design_zh, d) for d in (1, 2, 3)]
    observed = genotypes >= 0.0
    dosage = jnp.where(observed, genotypes, 0.0)
    cross = lax.dot_general(design, dosage, (((1,), (1,)), ((), ())), precision=HIGH)
    cross = cross + from_z(cross, 2)
    cross = (cross + from_x(cross, 2)) + (from_x(cross, 1) + from_x(cross, 3))
    total = None
    for d in designs:
        for k in range(2):
            part = lax.dot_general(d[k], d[k], (((1,), (1,)), ((), ())), precision=HIGH)
            total = part if total is None else total + part
    factor = jnp.linalg.cholesky(total[:count, :count])
    inverse = jax.scipy.linalg.cho_solve((factor, True), jnp.eye(count, dtype=jnp.float32))
    inverse = jnp.pad(inverse, ((0, PAD - count), (0, PAD - count)))
    coef = jnp.dot(inverse, cross, precision=HIGH)
    coef_far = from_z(coef, 1)

    def in_order(a, b):
        return jnp.concatenate([jnp.where(zh == 0, a, b), jnp.where(zh == 0, b, a)], axis=1)

    def my_half(value):
        return lax.dynamic_slice(value, (0, zl * half), (value.shape[0], half))

    own6 = terms(design, RIGHT)
    all6 = terms(jnp.concatenate([in_order(*designs[0])] + [my_half(d[0]) for d in designs], axis=1), RIGHT)
    near6 = terms(coef, LEFT)
    freq = frequencies(near6, own6)
    code = jnp.where(observed, dosage - 2.0 * freq, MISSING).astype(jnp.bfloat16)
    code, coef_far = lax.optimization_barrier((code, coef_far))
    up, down = from_z(code, 1), from_z(code, 3)
    near_half = my_half(code)
    near_rows = [near_half] + [from_x(near_half, d) for d in (1, 2, 3)]
    raw_columns, raw_rows = spreads(jnp.concatenate([near6, terms(coef_far, LEFT)], axis=1), all6)
    up, down, raw_columns, raw_rows = lax.optimization_barrier((up, down, raw_columns, raw_rows))
    far_same = jnp.where(zl == 0, up, down)
    far_other = jnp.where(zl == 0, down, up)
    far_half = my_half(far_same)
    far_rows = [far_half] + [from_x(far_half, d) for d in (1, 2, 3)]
    across = from_z(lax.optimization_barrier((code, up, down))[0], 2)
    count = 2 * code.shape[0]
    row_resid, row_spread = open_code(
        open_rows_kernel, (4, count, half), [], near_rows + far_rows + [raw_rows]
    )
    col_resid, col_spread = open_code(
        open_columns_kernel,
        (count, 2 * here),
        [jnp.reshape(zh, (1,)).astype(jnp.int32)],
        [code, across, far_same, far_other, raw_columns],
    )
    sums = None
    for step in (2, 1, 3, 0):
        d = (rows_at((y + step) % 4, zh) - x) % 4
        if sums is not None:
            d, _ = lax.optimization_barrier((d, give))
        numer = gram(lax.dynamic_index_in_dim(row_resid, d, 0, False), col_resid)
        denom = gram(lax.dynamic_index_in_dim(row_spread, d, 0, False), col_spread)
        both = jnp.stack([numer, denom])
        keep = lax.dynamic_slice(both, (0, 0, c * here), (2, half, here))
        give = lax.dynamic_slice(both, (0, 0, (1 - c) * here), (2, half, here))
        merged = keep + flip(give)
        if step:
            low = merged[1].astype(jnp.bfloat16)
            top = merged[0] * (low.astype(jnp.float32) / merged[1])
            merged = from_y(jnp.stack([top.astype(jnp.bfloat16), low]), 4 - step).astype(jnp.float32)
        sums = merged if sums is None else sums + merged
    return to_owner(sums[0] / (4.0 * sums[1]))


def solution(mesh):
    in_specs = (P("snp", "samp"), P(None, "samp"))
    out_specs = P("snp", "samp")
    return jax.shard_map(body, mesh=mesh, in_specs=in_specs, out_specs=out_specs, check_vma=False)
```

```python
import functools

import jax
import jax.numpy as jnp
from jax import lax
from jax.experimental import pallas as pl
from jax.experimental.pallas import tpu as pltpu
from jax.sharding import PartitionSpec as P

AXES = ("snp", "samp")
HIGH = lax.Precision.HIGHEST
MISSING = 4.0
PAD = 32
TILE = 256


def decode(snp, samp):
    return samp // 2, (snp // 2) % 4, samp % 2, snp // 8, snp % 2


def encode(x, y, zh, zl, c):
    return ((zl * 4 + y) * 2 + c) * 8 + x * 2 + zh


def pairs(where):
    return [(s * 8 + j, encode(*where(*decode(s, j)))) for s in range(16) for j in range(8)]


def move(value, where):
    return lax.ppermute(value, AXES, pairs(where))


def from_x(value, d):
    return move(value, lambda x, y, zh, zl, c: ((x - d) % 4, y, zh, zl, c))


def from_z(value, d):
    def where(x, y, zh, zl, c):
        z = (zh * 2 + zl - d) % 4
        return x, y, z // 2, z % 2, c

    return move(value, where)


def rows_at(y, zh):
    return zh * ((y % 2) * 2 + y // 2) + (1 - zh) * (y + y // 2 * (1 - y % 2 * 2))


def to_owner(value):
    def where(x, y, zh, zl, c):
        xi = rows_at(y, zh)
        return x, (xi % 2) * 2 + zh, c, xi // 2, zl

    return move(value, where)


LEFT = (0, 0, 1, 0, 2, 1)
RIGHT = (0, 1, 0, 2, 0, 1)


def terms_kernel(order, value, out):
    for k, part in enumerate(split_terms(value[...], order)):
        out[k * PAD : (k + 1) * PAD, :] = part


def terms(value, order):
    rows, columns = value.shape
    return pl.pallas_call(
        functools.partial(terms_kernel, order),
        out_shape=jax.ShapeDtypeStruct((rows * len(order), columns), jnp.bfloat16),
        compiler_params=pltpu.CompilerParams(vmem_limit_bytes=4 << 20),
        name="terms",
    )(value)


def frequencies(coef6, design6):
    fitted = lax.dot_general(coef6, design6, (((0,), (0,)), ((), ())), preferred_element_type=jnp.float32)
    return jnp.clip(0.5 * fitted, 0.02, 0.98)


def split_terms(a, order):
    parts = []
    for _ in range(3):
        parts.append(a.astype(jnp.bfloat16))
        a = a - parts[-1].astype(jnp.float32)
    return [parts[part] for part in order]


def clipped_spread(fitted):
    freq = jnp.clip(0.5 * fitted, 0.02, 0.98)
    square = freq * (1.0 - freq)
    return (square * lax.rsqrt(square)).astype(jnp.bfloat16)


def place(x, y, z, c):
    return ((z % 2) * 4 + y) * 2 + c, x * 2 + z // 2


def kinship_kernel(
    code, near6, right6, coef, out,
    across, near_in, far_in, coef_far, far6, col_resid, col_spread, row_resid, row_spread,
    product, flipped, y_out, y_in, send_sem, recv_sem,
):
    x, y, zh, zl, c = decode(lax.axis_index("snp"), lax.axis_index("samp"))
    z = zh * 2 + zl
    length, here = code.shape
    half = here // 2
    mine = pl.ds(pl.multiple_of(zl * half, half), half)

    to_x = [None] + [place((x + 4 - d) % 4, y, z, c) for d in (1, 2, 3)]
    to_y = [None] + [place(x, (y + d) % 4, z, c) for d in (1, 2, 3)]
    to_z = [None] + [place(x, y, (z + 4 - d) % 4, c) for d in (1, 2, 3)]
    core = place(x, y, z, 1 - c)

    def copy(n, source, target, device):
        return pltpu.make_async_remote_copy(
            src_ref=source,
            dst_ref=target,
            send_sem=send_sem.at[n],
            recv_sem=recv_sem.at[n],
            device_id=device,
            device_id_type=pl.DeviceIdType.MESH,
        )

    barrier = pltpu.get_barrier_semaphore()
    peers = to_x[1:] + to_y[1:] + to_z[1:] + [core]
    for peer in peers:
        pl.semaphore_signal(barrier, inc=1, device_id=peer, device_id_type=pl.DeviceIdType.MESH)
    pl.semaphore_wait(barrier, len(peers))

    far_coef = copy(0, coef, coef_far, to_z[1])
    from_up = copy(1, code, across.at[0], to_z[1])
    from_down = copy(2, code, across.at[1], to_z[3])
    from_two = copy(3, code, across.at[2], to_z[2])
    near = [copy(3 + d, code.at[:, mine], near_in.at[d - 1], to_x[d]) for d in (1, 2, 3)]
    far = [copy(6 + d, across.at[zl, :, mine], far_in.at[d - 1], to_x[d]) for d in (1, 2, 3)]
    far_coef.start()
    from_up.start()
    from_down.start()
    for one in near:
        one.start()

    def column_spreads(left, base):
        @pl.loop(0, length // TILE)
        def _(k):
            flat = left[:, pl.ds(pl.multiple_of(k * TILE, TILE), TILE)].T
            at = pl.ds(pl.multiple_of(base + k * TILE, TILE), TILE)
            for n in range(0, 2 * here, TILE):
                fitted = jnp.dot(flat, right6[:, n : n + TILE], preferred_element_type=jnp.float32)
                col_spread[at, n : n + TILE] = clipped_spread(fitted)

    def row_spreads(left, base):
        for d in range(4):
            first = 2 * here + d * half
            flat = right6[:, first : first + half].T

            @pl.loop(0, length // TILE)
            def _(k):
                fitted = jnp.dot(
                    flat, left[:, pl.ds(pl.multiple_of(k * TILE, TILE), TILE)], preferred_element_type=jnp.float32
                )
                row_spread[d, :, pl.ds(pl.multiple_of(base + k * TILE, TILE), TILE)] = clipped_spread(fitted)

    def open_columns(load, base, block):
        lanes = pl.ds(pl.multiple_of(block * here, here), here)

        @pl.loop(0, length // TILE)
        def _(k):
            value = load(pl.ds(pl.multiple_of(k * TILE, TILE), TILE))
            at = pl.ds(pl.multiple_of(base + k * TILE, TILE), TILE)
            zero = jnp.zeros_like(value)
            col_resid[at, lanes] = jnp.where(value < 3.0, value, zero)
            col_spread[at, lanes] = jnp.where(value < 3.0, col_spread[at, lanes], zero)

    def open_rows(load, base, d):
        @pl.loop(0, length // TILE)
        def _(k):
            value = load(pl.ds(pl.multiple_of(k * TILE, TILE), TILE)).T
            at = pl.ds(pl.multiple_of(base + k * TILE, TILE), TILE)
            zero = jnp.zeros_like(value)
            row_resid[d, :, at] = jnp.where(value < 3.0, value, zero)
            row_spread[d, :, at] = jnp.where(value < 3.0, row_spread[d, :, at], zero)

    column_spreads(near6, 0)
    row_spreads(near6, 0)
    far_coef.wait_recv()
    for k, part in enumerate(split_terms(coef_far[...], LEFT)):
        far6[k * PAD : (k + 1) * PAD, :] = part
    column_spreads(far6, length)
    row_spreads(far6, length)
    open_columns(lambda at: code[at, :], 0, zh)
    open_rows(lambda at: code[at, mine], 0, 0)
    from_up.wait_recv()
    from_down.wait_recv()
    for one in far:
        one.start()
    from_two.start()
    open_columns(lambda at: across[zl, at, :], length, zh)
    open_columns(lambda at: across[1 - zl, at, :], length, 1 - zh)
    open_rows(lambda at: across[zl, at, mine], length, 0)
    for d in (1, 2, 3):
        near[d - 1].wait_recv()
        open_rows(lambda at: near_in[d - 1, at, :], 0, d)
    for d in (1, 3, 2):
        far[d - 1].wait_recv()
        open_rows(lambda at: far_in[d - 1, at, :], length, d)
    from_two.wait_recv()
    open_columns(lambda at: across[2, at, :], 0, 1 - zh)

    flips = [copy(10 + s, product.at[s, 1 - c], flipped.at[s], core) for s in range(4)]
    sends = [None] + [copy(13 + s, y_out.at[s - 1], y_in.at[s - 1], to_y[s]) for s in (1, 2, 3)]

    def multiply(step):
        d = (rows_at((y + step) % 4, zh) + 4 - x) % 4
        for which, (left, right) in enumerate(((row_resid, col_resid), (row_spread, col_spread))):

            @pl.loop(0, 2 * here // TILE)
            def _(k):
                at = pl.ds(pl.multiple_of(k * TILE, TILE), TILE)
                inner = pl.ds(pl.multiple_of(k % 2 * TILE, TILE), TILE)
                product[step, k // 2, which, :, inner] = jnp.dot(
                    left[d], right[:, at], preferred_element_type=jnp.float32
                )

        flips[step].start()

    STRIP = 64

    def merge(step):
        flips[step].wait_recv()

        @pl.loop(0, half // STRIP)
        def _(k):
            at = pl.ds(pl.multiple_of(k * STRIP, STRIP), STRIP)
            numer = product[step, c, 0, at, :] + flipped[step, 0, at, :]
            denom = product[step, c, 1, at, :] + flipped[step, 1, at, :]
            low = denom.astype(jnp.bfloat16)
            y_out[step - 1, 0, at, :] = (numer * (low.astype(jnp.float32) / denom)).astype(jnp.bfloat16)
            y_out[step - 1, 1, at, :] = low

        sends[step].start()

    multiply(2)
    multiply(1)
    merge(2)
    multiply(3)
    merge(1)
    multiply(0)
    merge(3)
    flips[0].wait_recv()
    for s in (1, 3, 2):
        sends[s].wait_recv()

    @pl.loop(0, half // STRIP)
    def _(k):
        at = pl.ds(pl.multiple_of(k * STRIP, STRIP), STRIP)
        sums = []
        for which in range(2):
            total = product[0, c, which, at, :] + flipped[0, which, at, :]
            for s in range(3):
                total = total + y_in[s, which, at, :].astype(jnp.float32)
            sums.append(total)
        out[at, :] = sums[0] / (4.0 * sums[1])

    for one in [far_coef, from_up, from_down, from_two] + near + far + flips + sends[1:]:
        one.wait_send()


def kinship_blocks(code, near6, right6, coef):
    length, here = code.shape
    half = here // 2
    wide = lambda *shape: pltpu.VMEM(shape, jnp.float32)
    narrow = lambda *shape: pltpu.VMEM(shape, jnp.bfloat16)
    return pl.pallas_call(
        kinship_kernel,
        in_specs=[VMEM] * 4,
        out_specs=VMEM,
        out_shape=jax.ShapeDtypeStruct((half, here), jnp.float32),
        scratch_shapes=[
            narrow(3, length, here),
            narrow(3, length, half),
            narrow(3, length, half),
            wide(*coef.shape),
            narrow(*near6.shape),
            narrow(2 * length, 2 * here),
            narrow(2 * length, 2 * here),
            narrow(4, half, 2 * length),
            narrow(4, half, 2 * length),
            wide(4, 2, 2, half, here),
            wide(4, 2, half, here),
            narrow(3, 2, half, here),
            narrow(3, 2, half, here),
            pltpu.SemaphoreType.DMA((17,)),
            pltpu.SemaphoreType.DMA((17,)),
        ],
        compiler_params=pltpu.CompilerParams(
            collective_id=0, has_side_effects=True, vmem_limit_bytes=52 << 20
        ),
        name="kinship_blocks",
    )(code, near6, right6, coef)


VMEM = pl.BlockSpec(memory_space=pltpu.VMEM)


def body(genotypes, pcs):
    x, y, zh, zl, c = decode(lax.axis_index("snp"), lax.axis_index("samp"))
    here = genotypes.shape[1]
    half = here // 2
    count = pcs.shape[0] + 1
    design = jnp.concatenate([jnp.ones((1, here), jnp.float32), pcs, jnp.zeros((PAD - count, here), jnp.float32)], axis=0)
    design_zh = jnp.stack([design, from_z(design, 2)])
    designs = [design_zh] + [from_x(design_zh, d) for d in (1, 2, 3)]
    observed = genotypes >= 0.0
    dosage = jnp.where(observed, genotypes, 0.0)
    cross = lax.dot_general(design, dosage, (((1,), (1,)), ((), ())), precision=HIGH)
    cross = cross + from_z(cross, 2)
    cross = (cross + from_x(cross, 2)) + (from_x(cross, 1) + from_x(cross, 3))
    total = None
    for d in designs:
        for k in range(2):
            part = lax.dot_general(d[k], d[k], (((1,), (1,)), ((), ())), precision=HIGH)
            total = part if total is None else total + part
    factor = jnp.linalg.cholesky(total[:count, :count])
    inverse = jax.scipy.linalg.cho_solve((factor, True), jnp.eye(count, dtype=jnp.float32))
    inverse = jnp.pad(inverse, ((0, PAD - count), (0, PAD - count)))
    coef = jnp.dot(inverse, cross, precision=HIGH)

    def in_order(a, b):
        return jnp.concatenate([jnp.where(zh == 0, a, b), jnp.where(zh == 0, b, a)], axis=1)

    def my_half(value):
        return lax.dynamic_slice(value, (0, zl * half), (value.shape[0], half))

    own6 = terms(design, RIGHT)
    all6 = terms(jnp.concatenate([in_order(*designs[0])] + [my_half(d[0]) for d in designs], axis=1), RIGHT)
    near6 = terms(coef, LEFT)
    freq = frequencies(near6, own6)
    code = jnp.where(observed, dosage - 2.0 * freq, MISSING).astype(jnp.bfloat16)
    return to_owner(kinship_blocks(code, near6, all6, coef))


def solution(mesh):
    in_specs = (P("snp", "samp"), P(None, "samp"))
    out_specs = P("snp", "samp")
    return jax.shard_map(body, mesh=mesh, in_specs=in_specs, out_specs=out_specs, check_vma=False)
```

```python
import functools

import jax
import jax.numpy as jnp
from jax import lax
from jax.experimental import pallas as pl
from jax.experimental.pallas import tpu as pltpu
from jax.sharding import PartitionSpec as P

AXES = ("snp", "samp")
HIGH = lax.Precision.HIGHEST
MISSING = 4.0
PAD = 32
TILE = 256


def decode(snp, samp):
    return samp // 2, (snp // 2) % 4, samp % 2, snp // 8, snp % 2


def encode(x, y, zh, zl, c):
    return ((zl * 4 + y) * 2 + c) * 8 + x * 2 + zh


def pairs(where):
    return [(s * 8 + j, encode(*where(*decode(s, j)))) for s in range(16) for j in range(8)]


def move(value, where):
    return lax.ppermute(value, AXES, pairs(where))


def from_x(value, d):
    return move(value, lambda x, y, zh, zl, c: ((x - d) % 4, y, zh, zl, c))


def from_z(value, d):
    def where(x, y, zh, zl, c):
        z = (zh * 2 + zl - d) % 4
        return x, y, z // 2, z % 2, c

    return move(value, where)


def rows_at(y, zh):
    return zh * ((y % 2) * 2 + y // 2) + (1 - zh) * (y + y // 2 * (1 - y % 2 * 2))


LEFT = (0, 0, 1, 0, 2, 1)
RIGHT = (0, 1, 0, 2, 0, 1)


def terms_kernel(order, value, out):
    for k, part in enumerate(split_terms(value[...], order)):
        out[k * PAD : (k + 1) * PAD, :] = part


def terms(value, order):
    rows, columns = value.shape
    return pl.pallas_call(
        functools.partial(terms_kernel, order),
        out_shape=jax.ShapeDtypeStruct((rows * len(order), columns), jnp.bfloat16),
        compiler_params=pltpu.CompilerParams(vmem_limit_bytes=4 << 20),
        name="terms",
    )(value)


def frequencies(coef6, design6):
    fitted = lax.dot_general(coef6, design6, (((0,), (0,)), ((), ())), preferred_element_type=jnp.float32)
    return jnp.clip(0.5 * fitted, 0.02, 0.98)


def split_terms(a, order):
    parts = []
    for _ in range(3):
        parts.append(a.astype(jnp.bfloat16))
        a = a - parts[-1].astype(jnp.float32)
    return [parts[part] for part in order]


def clipped_spread(fitted):
    freq = jnp.clip(0.5 * fitted, 0.02, 0.98)
    square = freq * (1.0 - freq)
    return (square * lax.rsqrt(square)).astype(jnp.bfloat16)


def place(x, y, z, c):
    return ((z % 2) * 4 + y) * 2 + c, x * 2 + z // 2


def kinship_kernel(
    code, near6, right6, coef, out,
    across, near_in, far_in, coef_far, far6, col_resid, col_spread, row_resid, row_spread,
    product, flipped, y_out, y_in, done, send_sem, recv_sem,
):
    x, y, zh, zl, c = decode(lax.axis_index("snp"), lax.axis_index("samp"))
    z = zh * 2 + zl
    length, here = code.shape
    half = here // 2
    mine = pl.ds(pl.multiple_of(zl * half, half), half)
    other = pl.ds(pl.multiple_of((1 - zl) * half, half), half)
    top, bottom = pl.ds(0, length // 2), pl.ds(length // 2, length // 2)

    to_x = [None] + [place((x + 4 - d) % 4, y, z, c) for d in (1, 2, 3)]
    to_y = [None] + [place(x, (y + d) % 4, z, c) for d in (1, 2, 3)]
    to_z = [None] + [place(x, y, (z + 4 - d) % 4, c) for d in (1, 2, 3)]
    core = place(x, y, z, 1 - c)

    def copy(n, source, target, device):
        return pltpu.make_async_remote_copy(
            src_ref=source,
            dst_ref=target,
            send_sem=send_sem.at[n],
            recv_sem=recv_sem.at[n],
            device_id=device,
            device_id_type=pl.DeviceIdType.MESH,
        )

    xi = rows_at(y, zh)
    target = place(x, xi % 2 * 2 + zh, c * 2 + xi // 2, zl)
    source = place(x, rows_at(zl * 2 + y // 2, y % 2), y % 2 * 2 + c, zh)
    here_snp, here_samp = place(x, y, z, c)
    stays = jnp.logical_and(target[0] == here_snp, target[1] == here_samp)
    leaves = jnp.logical_not(stays)

    barrier = pltpu.get_barrier_semaphore()
    peers = to_x[1:] + to_y[1:] + [to_z[1], to_z[3], core]
    for peer in peers:
        pl.semaphore_signal(barrier, inc=1, device_id=peer, device_id_type=pl.DeviceIdType.MESH)

    @pl.when(leaves)
    def _():
        for peer in (target, source):
            pl.semaphore_signal(barrier, inc=1, device_id=peer, device_id_type=pl.DeviceIdType.MESH)

    pl.semaphore_wait(barrier, len(peers) + 2 * leaves.astype(jnp.int32))

    far_coef = copy(0, coef, coef_far, to_z[1])
    up_mine = copy(1, code.at[:, other], across.at[0, :, other], to_z[1])
    down_mine = copy(2, code.at[:, other], across.at[1, :, other], to_z[3])
    up_other = copy(3, code.at[:, mine], across.at[0, :, mine], to_z[1])
    down_other = copy(4, code.at[:, mine], across.at[1, :, mine], to_z[3])
    two_up = copy(5, across.at[0, :, mine], across.at[2, :, mine], to_z[1])
    two_down = copy(6, across.at[1, :, other], across.at[2, :, other], to_z[3])

    def along_x(n, first, into):
        return [
            copy(n, first, into.at[0], to_x[1]),
            copy(n + 1, first, into.at[2], to_x[3]),
            copy(n + 2, into.at[0, top], into.at[1, top], to_x[1]),
            copy(n + 3, into.at[2, bottom], into.at[1, bottom], to_x[3]),
        ]

    near = along_x(7, code.at[:, mine], near_in)
    far = along_x(11, across.at[zl, :, mine], far_in)
    for one in (up_mine, down_mine, near[0], near[1], far_coef, up_other, down_other):
        one.start()

    def column_spreads(left, base):
        @pl.loop(0, length // TILE)
        def _(k):
            flat = left[:, pl.ds(pl.multiple_of(k * TILE, TILE), TILE)].T
            at = pl.ds(pl.multiple_of(base + k * TILE, TILE), TILE)
            for n in range(0, 2 * here, TILE):
                fitted = jnp.dot(flat, right6[:, n : n + TILE], preferred_element_type=jnp.float32)
                col_spread[at, n : n + TILE] = clipped_spread(fitted)

    def row_spreads(left, base):
        for d in range(4):
            first = 2 * here + d * half
            flat = right6[:, first : first + half].T

            @pl.loop(0, length // TILE)
            def _(k):
                fitted = jnp.dot(
                    flat, left[:, pl.ds(pl.multiple_of(k * TILE, TILE), TILE)], preferred_element_type=jnp.float32
                )
                row_spread[d, :, pl.ds(pl.multiple_of(base + k * TILE, TILE), TILE)] = clipped_spread(fitted)

    def open_columns(load, base, block):
        lanes = pl.ds(pl.multiple_of(block * here, here), here)

        @pl.loop(0, length // TILE)
        def _(k):
            value = load(pl.ds(pl.multiple_of(k * TILE, TILE), TILE))
            at = pl.ds(pl.multiple_of(base + k * TILE, TILE), TILE)
            zero = jnp.zeros_like(value)
            col_resid[at, lanes] = jnp.where(value < 3.0, value, zero)
            col_spread[at, lanes] = jnp.where(value < 3.0, col_spread[at, lanes], zero)

    def open_rows(load, base, d):
        @pl.loop(0, length // TILE)
        def _(k):
            value = load(pl.ds(pl.multiple_of(k * TILE, TILE), TILE)).T
            at = pl.ds(pl.multiple_of(base + k * TILE, TILE), TILE)
            zero = jnp.zeros_like(value)
            row_resid[d, :, at] = jnp.where(value < 3.0, value, zero)
            row_spread[d, :, at] = jnp.where(value < 3.0, row_spread[d, :, at], zero)

    column_spreads(near6, 0)
    row_spreads(near6, 0)
    far_coef.wait_recv()
    for k, part in enumerate(split_terms(coef_far[...], LEFT)):
        far6[k * PAD : (k + 1) * PAD, :] = part
    column_spreads(far6, length)
    row_spreads(far6, length)
    open_columns(lambda at: code[at, :], 0, zh)
    open_rows(lambda at: code[at, mine], 0, 0)
    up_mine.wait_recv()
    down_mine.wait_recv()
    for one in (far[0], far[1], two_up):
        one.start()
    near[0].wait_recv()
    near[2].start()
    near[1].wait_recv()
    near[3].start()
    open_rows(lambda at: across[zl, at, mine], length, 0)
    open_rows(lambda at: near_in[0, at, :], 0, 1)
    open_rows(lambda at: near_in[2, at, :], 0, 3)
    down_other.wait_recv()
    two_down.start()
    far[0].wait_recv()
    far[2].start()
    far[1].wait_recv()
    far[3].start()
    up_other.wait_recv()
    open_columns(lambda at: across[zl, at, :], length, zh)
    open_columns(lambda at: across[1 - zl, at, :], length, 1 - zh)
    open_rows(lambda at: far_in[0, at, :], length, 1)
    open_rows(lambda at: far_in[2, at, :], length, 3)
    near[2].wait_recv()
    near[3].wait_recv()
    open_rows(lambda at: near_in[1, at, :], 0, 2)
    two_up.wait_recv()
    two_down.wait_recv()
    open_columns(lambda at: across[2, at, :], 0, 1 - zh)
    far[2].wait_recv()
    far[3].wait_recv()
    open_rows(lambda at: far_in[1, at, :], length, 2)

    strips = [pl.ds(t * (half // 2), half // 2) for t in range(2)]
    flips = [copy(15 + s, product.at[s, 1 - c], flipped.at[s], core) for s in range(4)]
    sends = [None] + [
        [copy(17 + s * 2 + t, y_out.at[s - 1, :, strips[t]], y_in.at[s - 1, :, strips[t]], to_y[s]) for t in range(2)]
        for s in (1, 2, 3)
    ]
    last = [copy(25 + t, done.at[strips[t]], out.at[strips[t]], target) for t in range(2)]

    def multiply(step):
        d = (rows_at((y + step) % 4, zh) + 4 - x) % 4
        for which, (left, right) in enumerate(((row_resid, col_resid), (row_spread, col_spread))):

            @pl.loop(0, 2 * here // TILE)
            def _(k):
                at = pl.ds(pl.multiple_of(k * TILE, TILE), TILE)
                inner = pl.ds(pl.multiple_of(k % 2 * TILE, TILE), TILE)
                product[step, k // 2, which, :, inner] = jnp.dot(
                    left[d], right[:, at], preferred_element_type=jnp.float32
                )

        flips[step].start()

    STRIP = 64

    def merge(step):
        flips[step].wait_recv()

        @pl.loop(0, half // STRIP)
        def _(k):
            at = pl.ds(pl.multiple_of(k * STRIP, STRIP), STRIP)
            numer = product[step, c, 0, at, :] + flipped[step, 0, at, :]
            denom = product[step, c, 1, at, :] + flipped[step, 1, at, :]
            low = denom.astype(jnp.bfloat16)
            y_out[step - 1, 0, at, :] = (numer * (low.astype(jnp.float32) / denom)).astype(jnp.bfloat16)
            y_out[step - 1, 1, at, :] = low

        for one in sends[step]:
            one.start()

    multiply(2)
    multiply(1)
    merge(2)
    multiply(3)
    merge(1)
    multiply(0)
    merge(3)
    flips[0].wait_recv()
    for t in range(2):
        for s in (2, 1, 3):
            sends[s][t].wait_recv()

        @pl.loop(0, half // 2 // STRIP)
        def _(k):
            at = pl.ds(pl.multiple_of(t * (half // 2) + k * STRIP, STRIP), STRIP)
            sums = []
            for which in range(2):
                total = product[0, c, which, at, :] + flipped[0, which, at, :]
                for s in range(3):
                    total = total + y_in[s, which, at, :].astype(jnp.float32)
                sums.append(total)
            done[at, :] = sums[0] / (4.0 * sums[1])

        @pl.when(leaves)
        def _():
            last[t].start()

    @pl.when(stays)
    def _():
        out[...] = done[...]

    moved = [far_coef, up_mine, down_mine, up_other, down_other, two_up, two_down]
    for one in moved + near + far + flips + sends[1] + sends[2] + sends[3]:
        one.wait_send()

    @pl.when(leaves)
    def _():
        for one in last:
            one.wait()


def kinship_blocks(code, near6, right6, coef):
    length, here = code.shape
    half = here // 2
    wide = lambda *shape: pltpu.VMEM(shape, jnp.float32)
    narrow = lambda *shape: pltpu.VMEM(shape, jnp.bfloat16)
    return pl.pallas_call(
        kinship_kernel,
        in_specs=[VMEM] * 4,
        out_specs=VMEM,
        out_shape=jax.ShapeDtypeStruct((half, here), jnp.float32),
        scratch_shapes=[
            narrow(3, length, here),
            narrow(3, length, half),
            narrow(3, length, half),
            wide(*coef.shape),
            narrow(*near6.shape),
            narrow(2 * length, 2 * here),
            narrow(2 * length, 2 * here),
            narrow(4, half, 2 * length),
            narrow(4, half, 2 * length),
            wide(4, 2, 2, half, here),
            wide(4, 2, half, here),
            narrow(3, 2, half, here),
            narrow(3, 2, half, here),
            wide(half, here),
            pltpu.SemaphoreType.DMA((27,)),
            pltpu.SemaphoreType.DMA((27,)),
        ],
        compiler_params=pltpu.CompilerParams(
            collective_id=0, has_side_effects=True, vmem_limit_bytes=52 << 20
        ),
        name="kinship_blocks",
    )(code, near6, right6, coef)


VMEM = pl.BlockSpec(memory_space=pltpu.VMEM)


def body(genotypes, pcs):
    x, y, zh, zl, c = decode(lax.axis_index("snp"), lax.axis_index("samp"))
    here = genotypes.shape[1]
    half = here // 2
    count = pcs.shape[0] + 1
    design = jnp.concatenate([jnp.ones((1, here), jnp.float32), pcs, jnp.zeros((PAD - count, here), jnp.float32)], axis=0)
    design_zh = jnp.stack([design, from_z(design, 2)])
    designs = [design_zh] + [from_x(design_zh, d) for d in (1, 2, 3)]
    observed = genotypes >= 0.0
    dosage = jnp.where(observed, genotypes, 0.0)
    cross = lax.dot_general(design, dosage, (((1,), (1,)), ((), ())), precision=HIGH)
    cross = cross + from_z(cross, 2)
    cross = (cross + from_x(cross, 2)) + (from_x(cross, 1) + from_x(cross, 3))
    total = None
    for d in designs:
        for k in range(2):
            part = lax.dot_general(d[k], d[k], (((1,), (1,)), ((), ())), precision=HIGH)
            total = part if total is None else total + part
    factor = jnp.linalg.cholesky(total[:count, :count])
    inverse = jax.scipy.linalg.cho_solve((factor, True), jnp.eye(count, dtype=jnp.float32))
    inverse = jnp.pad(inverse, ((0, PAD - count), (0, PAD - count)))
    coef = jnp.dot(inverse, cross, precision=HIGH)

    def in_order(a, b):
        return jnp.concatenate([jnp.where(zh == 0, a, b), jnp.where(zh == 0, b, a)], axis=1)

    def my_half(value):
        return lax.dynamic_slice(value, (0, zl * half), (value.shape[0], half))

    own6 = terms(design, RIGHT)
    all6 = terms(jnp.concatenate([in_order(*designs[0])] + [my_half(d[0]) for d in designs], axis=1), RIGHT)
    near6 = terms(coef, LEFT)
    freq = frequencies(near6, own6)
    code = jnp.where(observed, dosage - 2.0 * freq, MISSING).astype(jnp.bfloat16)
    return kinship_blocks(code, near6, all6, coef)


def solution(mesh):
    in_specs = (P("snp", "samp"), P(None, "samp"))
    out_specs = P("snp", "samp")
    return jax.shard_map(body, mesh=mesh, in_specs=in_specs, out_specs=out_specs, check_vma=False)
```
